256 devices in a mesh: row: 8 (over x_lo, y), col: 32 (over z, x_hi, core).
Axes of the slice: x: 4 (x_hi: 2, x_lo: 2; x = x_hi * 2 + x_lo), y: 4, z: 8, core: 2. Of those that a mesh axis runs over, the one named last changes fastest.
Arguments:
- amplitudes: bfloat16 [32768, 4096], P('col', 'row'), may hold values from -6 to 6
- integrals: bfloat16 [4096, 8192], P('col', 'row'), may hold values from -0.25 to 0.25
- sym_mask: int32 [32, 64], replicated, may hold values from 0 to 1, as said below
Outputs:
- ladder: bfloat16 [32768, 8192], P('col', 'row')
The draws below stay inside these ranges and needn't reach their ends.
Inputs may be any that keep to these rules, and one draw needn't show every extreme that they name: sym_mask[k, a] is 1 exactly when cd tile k and ab tile a carry the same one of 8 irreducible representations; among the 8 ab tiles of one index of row, at most 2 carry the same representation.
All inputs are finite; a program needn't handle non-finite values.
Results may differ from the reference program's by a relative error of at most 0.001.
Values may be sent and summed in bfloat16 or wider, within the bound.
No kernel may reach another device: no remote copies, remote signals or barrier semaphores. Data moves between devices by JAX's collectives and lax.ppermute only.
A program may use at most 64 MiB of HBM per device.

```python
import jax
import jax.numpy as jnp

TILE = 128
AB_TILES = 8
NIJ = 32768
NCD = 4096
NAB = 8192
N_ROW = 8
N_COL = 32


def draw_sym_mask(key, part):
    table = jnp.array([0, 0, 0, 0, 1, 1, 1, 2, 2, 3, 3, 4, 5, 5, 6, 7], jnp.int32)
    cd_irrep = table[jax.random.randint(jax.random.fold_in(key, 11), (N_COL,), 0, 16)]

    def one_block(index):
        block_key = jax.random.fold_in(jax.random.fold_in(key, 23), index)
        first = cd_irrep[index % N_COL]
        others = (first + 1 + jax.random.permutation(jax.random.fold_in(block_key, 1), 7)[:AB_TILES - 2].astype(jnp.int32)) % 8
        labels = jnp.concatenate([jnp.stack([first, first]), others.astype(jnp.int32)])
        return labels[jax.random.permutation(jax.random.fold_in(block_key, 2), AB_TILES)]
    ab_irrep = jax.vmap(one_block)(jnp.arange(N_ROW, dtype=jnp.int32)).reshape(-1)
    return (cd_irrep[:, None] == ab_irrep[None, :]).astype(jnp.int32)


def steps_of(rng, shape, split, least, largest):
    loudness = 1.0
    for axis_at, blocks in split:
        draws = jax.random.uniform(jax.random.fold_in(jax.random.fold_in(rng, 6), axis_at), (blocks,), jnp.float32, least / len(split), largest / len(split))
        loudness = loudness * jnp.repeat(jnp.exp(draws), shape[axis_at] // blocks).reshape((-1,) + (1,) * (len(shape) - 1 - axis_at))
    return loudness


def scatter_about(stream_key, shape, deviation, limit, pieces=(), held_as=jnp.bfloat16):
    result = jax.random.normal(stream_key, shape, jnp.float32) * deviation
    if len(pieces) > 0:
        result = steps_of(stream_key, shape, pieces, -0.22, 0.18) * result
    return jnp.clip(result, min=-limit, max=limit).astype(held_as)


def setup_inputs(seed: int = 0) -> dict:
    keys = jax.random.split(jax.random.key(seed), 4)
    amplitudes = scatter_about(keys[0], (NIJ, NCD), 1.0, 6.0, ((0, 32), (1, 8)))
    integrals = scatter_about(keys[1], (NCD, NAB), (NCD // 8) ** -0.5, 0.25, ((0, 32), (1, 8)))
    sym_mask = draw_sym_mask(jax.random.fold_in(keys[3], 71), 0)
    return {"amplitudes": amplitudes, "integrals": integrals, "sym_mask": sym_mask}


def reference(amplitudes, integrals, sym_mask):
    expanded = jnp.repeat(jnp.repeat(sym_mask, TILE, axis=0), TILE, axis=1)
    masked = integrals * expanded.astype(jnp.bfloat16)
    return jnp.dot(amplitudes, masked, preferred_element_type=jnp.float32).astype(jnp.bfloat16)
```

```python
import jax
import jax.numpy as jnp
from jax import lax
from jax.experimental import pallas as pl
from jax.experimental.pallas import tpu as pltpu
from jax.sharding import PartitionSpec as P

TILE = 128
AB = 8
VMEM = pltpu.VMEM
SMEM = pltpu.SMEM


def spec(space):
    return pl.BlockSpec(memory_space=space)


def row_permute(value, flip):
    return lax.ppermute(value, "row", [(i, i ^ flip) for i in range(8)])


def pack_kernel(where_ref, mask_ref, v_ref, out_ref):
    c, r = where_ref[0], where_ref[1]
    first, last, found = jnp.int32(0), jnp.int32(0), jnp.int32(0)
    for j in range(AB):
        hit = mask_ref[c, r * AB + j] > 0
        first = jnp.where(jnp.logical_and(hit, found == 0), j, first)
        last = jnp.where(hit, j, last)
        found = jnp.where(hit, 1, found)
    zero = jnp.zeros((TILE, TILE), v_ref.dtype)
    one = v_ref[:, pl.ds(pl.multiple_of(first * TILE, TILE), TILE)]
    two = v_ref[:, pl.ds(pl.multiple_of(last * TILE, TILE), TILE)]
    out_ref[:, :TILE] = jnp.where(found > 0, one, zero)
    out_ref[:, TILE:] = jnp.where(jnp.logical_and(found > 0, last != first), two, zero)


def table_kernel(where_ref, mask_ref, out_ref):
    r = where_ref[1]

    @pl.loop(0, 32)
    def _(k):
        first, last = jnp.int32(AB), jnp.int32(0)
        for j in range(AB):
            hit = mask_ref[k, r * AB + j] > 0
            first = jnp.where(hit, jnp.minimum(first, j), first)
            last = jnp.where(hit, j, last)
        first = jnp.where(first == AB, 0, first)
        out_ref[0, k] = first
        out_ref[1, k] = last


def add_block(where_ref, table_ref, mine, other, t_ref, z, acc_ref, rows, base):
    xh = lax.rem(lax.div(where_ref[0], 2), 2)
    co = lax.rem(where_ref[0], 2)
    for t in range(4):
        k = z * 4 + t
        j = lax.rem(xh + (t >> 1), 2)
        own = co == (t & 1)
        slab = jnp.where(own, mine[z, j], other[z, j])
        left = pl.ds(pl.multiple_of(table_ref[0, k] * TILE, TILE), TILE)
        right = pl.ds(pl.multiple_of(table_ref[1, k] * TILE, TILE), TILE)
        for m in range(base, base + rows, 256):
            size = min(256, base + rows - m)
            p = jnp.dot(
                t_ref[m - base : m - base + size, t * TILE : (t + 1) * TILE],
                slab,
                preferred_element_type=jnp.float32,
            )
            acc_ref[m : m + size, left] += p[:, :TILE]
            acc_ref[m : m + size, right] += p[:, TILE:]


def first_kernel(where_ref, table_ref, mine, other, *refs):
    *ts, acc_ref = refs
    acc_ref[...] = jnp.zeros_like(acc_ref)
    for t_ref, flip in zip(ts, (0, 4, 1, 3)):
        add_block(where_ref, table_ref, mine, other, t_ref, where_ref[1] ^ flip, acc_ref, 1024, 0)


def second_kernel(where_ref, table_ref, mine, other, acc_in, *refs):
    *ts, acc_ref = refs
    for t_ref, flip in zip(ts, (7, 5, 2)):
        add_block(where_ref, table_ref, mine, other, t_ref, where_ref[1] ^ flip, acc_ref, 1024, 0)


THIRDS = (352, 336, 336)


def third_kernel(where_ref, table_ref, mine, other, acc_ref, ta, tb, tc, out_ref):
    base = 0
    for t_ref, n in zip((ta, tb, tc), THIRDS):
        add_block(where_ref, table_ref, mine, other, t_ref, where_ref[1] ^ 6, acc_ref, n, base)
        out_ref[base : base + n] = acc_ref[base : base + n].astype(out_ref.dtype)
        base += n


def params():
    return pltpu.CompilerParams(vmem_limit_bytes=40 * 1024 * 1024)


def shards(amps, integrals, sym_mask):
    r, c = lax.axis_index("row"), lax.axis_index("col")
    where = jnp.stack([c, r]).astype(jnp.int32)
    packed = pl.pallas_call(
        pack_kernel,
        in_specs=[spec(SMEM), spec(SMEM), spec(VMEM)],
        out_specs=spec(VMEM),
        out_shape=jax.ShapeDtypeStruct((TILE, 2 * TILE), jnp.bfloat16),
        name="pack",
    )(where, sym_mask, integrals)
    table = pl.pallas_call(
        table_kernel,
        in_specs=[spec(SMEM), spec(SMEM)],
        out_specs=spec(SMEM),
        out_shape=jax.ShapeDtypeStruct((2, 32), jnp.int32),
        name="table",
    )(where, sym_mask)
    across = lax.ppermute(packed, "col", [(i, i ^ 2) for i in range(32)])
    pair = jnp.stack([packed, across])
    groups = [[z * 4 + k for z in range(8)] for k in range(4)]
    mine = lax.all_gather(pair, "col", axis=0, tiled=False, axis_index_groups=groups)
    other = lax.ppermute(mine, "col", [(i, i ^ 1) for i in range(32)])

    p1 = row_permute(amps, 4)
    q1 = row_permute(amps, 1)
    w1 = row_permute(amps, 3)
    pw = row_permute(w1, 4)
    qp = row_permute(p1, 1)
    wq = row_permute(q1, 3)
    a, b, _ = THIRDS
    last = (row_permute(wq[:a], 4), row_permute(pw[a : a + b], 1), row_permute(qp[a + b :], 3))

    acc_shape = jax.ShapeDtypeStruct((1024, 1024), jnp.float32)
    acc = pl.pallas_call(
        first_kernel,
        in_specs=[spec(SMEM), spec(SMEM)] + [spec(VMEM)] * 6,
        out_specs=spec(VMEM),
        out_shape=acc_shape,
        compiler_params=params(),
        cost_estimate=pl.CostEstimate(flops=2 * 1024 * 2048 * 1024, bytes_accessed=1, transcendentals=0),
        name="first",
    )(where, table, mine, other, amps, p1, q1, w1)
    acc = pl.pallas_call(
        second_kernel,
        in_specs=[spec(SMEM), spec(SMEM)] + [spec(VMEM)] * 6,
        out_specs=spec(VMEM),
        out_shape=acc_shape,
        input_output_aliases={4: 0},
        compiler_params=params(),
        cost_estimate=pl.CostEstimate(flops=2 * 1024 * 1536 * 1024, bytes_accessed=1, transcendentals=0),
        name="second",
    )(where, table, mine, other, acc, pw, qp, wq)
    return pl.pallas_call(
        third_kernel,
        in_specs=[spec(SMEM), spec(SMEM)] + [spec(VMEM)] * 6,
        out_specs=spec(VMEM),
        out_shape=jax.ShapeDtypeStruct((1024, 1024), jnp.bfloat16),
        compiler_params=params(),
        name="third",
    )(where, table, mine, other, acc, *last)


def solution(mesh):
    placed = (P("col", "row"), P("col", "row"), P())
    return jax.shard_map(
        shards, mesh=mesh, in_specs=placed, out_specs=P("col", "row"), check_vma=False
    )
```

```python
import jax
import jax.numpy as jnp
from jax import lax
from jax.experimental import pallas as pl
from jax.experimental.pallas import tpu as pltpu
from jax.sharding import PartitionSpec as P

TILE = 128
AB = 8
PARTS = (352, 304, 368)
VMEM = pltpu.VMEM
SMEM = pltpu.SMEM
BF16 = jnp.bfloat16
barrier = lax.optimization_barrier


def spec(space):
    return pl.BlockSpec(memory_space=space)


def row_flip(value, flip):
    return lax.ppermute(value, "row", [(i, i ^ flip) for i in range(8)])


def col_flip(value, flip):
    return lax.ppermute(value, "col", [(i, i ^ flip) for i in range(32)])


def z_step(value, by):
    return lax.ppermute(
        value, "col", [(i, (i + (4 * by if i % 2 == 0 else -4 * by)) % 32) for i in range(32)]
    )


def place():
    return lax.axis_index("row"), lax.axis_index("col")


def tile_at(index):
    return pl.ds(pl.multiple_of(index * TILE, TILE), TILE)


def pack_kernel(mask_ref, v_ref, out_ref):
    r, c = place()
    first, last, found = jnp.int32(0), jnp.int32(0), jnp.int32(0)
    for j in range(AB):
        hit = mask_ref[c, r * AB + j] > 0
        first = jnp.where(jnp.logical_and(hit, found == 0), j, first)
        last = jnp.where(hit, j, last)
        found = jnp.where(hit, 1, found)
    zero = jnp.zeros((TILE, TILE), v_ref.dtype)
    out_ref[:, :TILE] = jnp.where(found > 0, v_ref[:, tile_at(first)], zero)
    out_ref[:, TILE:] = jnp.where(last != first, v_ref[:, tile_at(last)], zero)


def table_kernel(mask_ref, out_ref):
    r, _ = place()

    @pl.loop(0, 32)
    def _(k):
        first, last = jnp.int32(AB), jnp.int32(0)
        for j in range(AB):
            hit = mask_ref[k, r * AB + j] > 0
            first = jnp.where(hit, jnp.minimum(first, j), first)
            last = jnp.where(hit, j, last)
        out_ref[0, k] = jnp.where(first == AB, 0, first)
        out_ref[1, k] = last


def join_kernel(a, b, out_ref):
    n = out_ref.shape[0] // 2
    out_ref[:n] = a[...].reshape((n,) + out_ref.shape[1:])
    out_ref[n:] = b[...].reshape((n,) + out_ref.shape[1:])


def three_kernel(a, b, c, out_ref):
    for i, ref in enumerate((a, b, c)):
        out_ref[4 * i : 4 * i + 4] = ref[...]


def dense_kernel(table_ref, quad, r1, r2, r3, r4, theirs, out_ref):
    _, c = place()
    co, xh, z = lax.rem(c, 2), lax.rem(lax.div(c, 2), 2), lax.div(c, 4)
    way = 1 - 2 * co
    out_ref[...] = jnp.zeros_like(out_ref)
    for ref, core, shift in (
        (quad, co, 0),
        (r1, co, -way),
        (r2, co, -2 * way),
        (r3, co, -3 * way),
        (r4, co, 4),
        (theirs.at[0:4], 1 - co, way),
        (theirs.at[4:8], 1 - co, 2 * way),
        (theirs.at[8:12], 1 - co, 3 * way),
    ):
        plane = lax.rem(z + shift + 8, 8)
        for j in range(4):
            k = plane * 4 + (xh ^ (j & 1)) * 2 + (core ^ (j >> 1))
            rows = tile_at(k)
            out_ref[rows, tile_at(table_ref[1, k])] = ref[j, :, TILE:]
            out_ref[rows, tile_at(table_ref[0, k])] = ref[j, :, :TILE]


def block_rows(dense_ref, flip):
    z = place()[0] ^ flip
    return dense_ref.at[pl.ds(pl.multiple_of(z * 512, 512), 512)]


def dot(a, b):
    return jnp.dot(a, b, preferred_element_type=jnp.float32)


def total(ts, blocks, cols):
    return sum(dot(t[...], block[:, cols]) for t, block in zip(ts, blocks))


def first_kernel(dense_ref, own, p1, q1, w1, acc_ref):
    blocks = [block_rows(dense_ref, flip) for flip in (0, 4, 1, 3)]
    for col in (0, 512):
        cols = slice(col, col + 512)
        acc_ref[:, cols] = total((own, p1, q1, w1), blocks, cols)


def second_kernel(dense_ref, acc_in, pw, qp, wq, acc_ref):
    blocks = [block_rows(dense_ref, flip) for flip in (7, 5, 2)]
    for col in (0, 512):
        cols = slice(col, col + 512)
        acc_ref[:, cols] = acc_in[:, cols] + total((pw, qp, wq), blocks, cols)


def third_kernel(dense_ref, acc_ref, ta, tb, tc, out_ref, held, sems):
    block = block_rows(dense_ref, 6)
    copies = []
    for col in (0, 512):
        cols = slice(col, col + 512)
        base = 0
        for t_ref, n in zip((ta, tb, tc), PARTS):
            rows = slice(base, base + n)
            held[rows, cols] = (acc_ref[rows, cols] + dot(t_ref[...], block[:, cols])).astype(held.dtype)
            copy = pltpu.make_async_copy(held.at[rows, cols], out_ref.at[rows, cols], sems.at[len(copies)])
            copy.start()
            copies.append(copy)
            base += n
    for copy in copies:
        copy.wait()


def call(kernel, args, shape, dtype, name, table=False, out_space=VMEM, flops=1000, limit=8, **more):
    return pl.pallas_call(
        kernel,
        in_specs=[spec(SMEM)] * table + [spec(VMEM)] * (len(args) - table),
        out_specs=spec(out_space),
        out_shape=jax.ShapeDtypeStruct(shape, dtype),
        compiler_params=pltpu.CompilerParams(vmem_limit_bytes=limit * 1024 * 1024),
        cost_estimate=pl.CostEstimate(flops=flops, bytes_accessed=1000, transcendentals=0),
        name=name,
        **more,
    )(*args)


def shards(amps, integrals, sym_mask):
    q1, w1 = row_flip(amps, 1), row_flip(amps, 3)
    packed = call(
        pack_kernel, (sym_mask, integrals), (TILE, 2 * TILE), BF16, "pack", table=True, limit=60
    )
    table = call(table_kernel, (sym_mask,), (2, 32), jnp.int32, "table", table=True, out_space=SMEM)

    sent, packed = barrier((amps, packed))
    p1 = row_flip(sent, 4)
    pair = call(join_kernel, (packed, col_flip(packed, 2)), (2, TILE, 2 * TILE), BF16, "pair", flops=20000000000)
    quad = call(join_kernel, (pair, col_flip(pair, 1)), (4, TILE, 2 * TILE), BF16, "quad")
    r1, r2 = z_step(quad, 1), z_step(quad, 2)
    p1, q1, w1 = barrier((p1, q1, w1))
    r3, r4 = z_step(r2, 1), z_step(r2, 2)
    theirs = col_flip(call(three_kernel, (r1, r2, r3), (12, TILE, 2 * TILE), BF16, "three"), 1)
    dense = call(
        dense_kernel, (table, quad, r1, r2, r3, r4, theirs), (4096, 1024), BF16, "dense", table=True, flops=2000000000
    )

    pw, qp, wq = row_flip(w1, 4), row_flip(p1, 1), row_flip(q1, 3)
    acc = call(first_kernel, (dense, amps, p1, q1, w1), (1024, 1024), jnp.float32, "first")
    wq, pw, qp = (barrier((acc, v))[1] for v in (wq, pw, qp))
    a, b, _ = PARTS
    last = (row_flip(wq[:a], 4), row_flip(pw[a : a + b], 1), row_flip(qp[a + b :], 3))
    acc = call(
        second_kernel, (dense, acc, pw, qp, wq), (1024, 1024), jnp.float32, "second",
        input_output_aliases={1: 0},
    )
    return call(
        third_kernel, (dense, acc, *last), (1024, 1024), BF16, "third", out_space=pl.ANY,
        scratch_shapes=[VMEM((1024, 1024), BF16), pltpu.SemaphoreType.DMA((6,))],
    )


def solution(mesh):
    placed = (P("col", "row"), P("col", "row"), P())
    return jax.shard_map(
        shards, mesh=mesh, in_specs=placed, out_specs=P("col", "row"), check_vma=False
    )
```

```python
import jax
import jax.numpy as jnp
from jax import lax
from jax.experimental import pallas as pl
from jax.experimental.pallas import tpu as pltpu
from jax.sharding import PartitionSpec as P

TILE = 128
AB = 8
PARTS = (352, 304, 368)
VMEM = pltpu.VMEM
SMEM = pltpu.SMEM
BF16 = jnp.bfloat16
barrier = lax.optimization_barrier


def spec(space):
    return pl.BlockSpec(memory_space=space)


def row_flip(value, flip):
    return lax.ppermute(value, "row", [(i, i ^ flip) for i in range(8)])


def col_flip(value, flip):
    return lax.ppermute(value, "col", [(i, i ^ flip) for i in range(32)])


def z_step(value, by):
    return lax.ppermute(
        value, "col", [(i, (i + (4 * by if i % 2 == 0 else -4 * by)) % 32) for i in range(32)]
    )


def place():
    return lax.axis_index("row"), lax.axis_index("col")


def tile_at(index):
    return pl.ds(pl.multiple_of(index * TILE, TILE), TILE)


def pack_kernel(mask_ref, v_ref, out_ref):
    r, c = place()
    first, last, found = jnp.int32(0), jnp.int32(0), jnp.int32(0)
    for j in range(AB):
        hit = mask_ref[c, r * AB + j] > 0
        first = jnp.where(jnp.logical_and(hit, found == 0), j, first)
        last = jnp.where(hit, j, last)
        found = jnp.where(hit, 1, found)
    zero = jnp.zeros((TILE, TILE), v_ref.dtype)
    out_ref[:, :TILE] = jnp.where(found > 0, v_ref[:, tile_at(first)], zero)
    out_ref[:, TILE:] = jnp.where(last != first, v_ref[:, tile_at(last)], zero)


def table_kernel(mask_ref, out_ref):
    r, _ = place()

    @pl.loop(0, 32)
    def _(k):
        first, last = jnp.int32(AB), jnp.int32(0)
        for j in range(AB):
            hit = mask_ref[k, r * AB + j] > 0
            first = jnp.where(hit, jnp.minimum(first, j), first)
            last = jnp.where(hit, j, last)
        out_ref[0, k] = jnp.where(first == AB, 0, first)
        out_ref[1, k] = last


def join_kernel(a, b, out_ref):
    n = out_ref.shape[0] // 2
    out_ref[:n] = a[...].reshape((n,) + out_ref.shape[1:])
    out_ref[n:] = b[...].reshape((n,) + out_ref.shape[1:])


def three_kernel(a, b, c, out_ref):
    for i, ref in enumerate((a, b, c)):
        out_ref[4 * i : 4 * i + 4] = ref[...]


def dense_kernel(table_ref, quad, r1, r2, r3, r4, theirs, out_ref):
    _, c = place()
    co, xh, z = lax.rem(c, 2), lax.rem(lax.div(c, 2), 2), lax.div(c, 4)
    way = 1 - 2 * co
    out_ref[...] = jnp.zeros_like(out_ref)
    for ref, core, shift in (
        (quad, co, 0),
        (r1, co, -way),
        (r2, co, -2 * way),
        (r3, co, -3 * way),
        (r4, co, 4),
        (theirs.at[0:4], 1 - co, way),
        (theirs.at[4:8], 1 - co, 2 * way),
        (theirs.at[8:12], 1 - co, 3 * way),
    ):
        plane = lax.rem(z + shift + 8, 8)
        for j in range(4):
            k = plane * 4 + (xh ^ (j & 1)) * 2 + (core ^ (j >> 1))
            rows = tile_at(k)
            out_ref[rows, tile_at(table_ref[1, k])] = ref[j, :, TILE:]
            out_ref[rows, tile_at(table_ref[0, k])] = ref[j, :, :TILE]


def block_rows(dense_ref, flip):
    z = place()[0] ^ flip
    return dense_ref.at[pl.ds(pl.multiple_of(z * 512, 512), 512)]


def dot(a, b):
    return jnp.dot(a, b, preferred_element_type=jnp.float32)


def total(ts, blocks, cols):
    return sum(dot(t[...], block[:, cols]) for t, block in zip(ts, blocks))


def first_kernel(dense_ref, own, p1, q1, w1, acc_ref):
    blocks = [block_rows(dense_ref, flip) for flip in (0, 4, 1, 3)]
    for col in (0, 512):
        cols = slice(col, col + 512)
        acc_ref[:, cols] = total((own, p1, q1, w1), blocks, cols)


def second_kernel(dense_ref, acc_in, pw, qp, wq, acc_ref):
    blocks = [block_rows(dense_ref, flip) for flip in (7, 5, 2)]
    for col in (0, 512):
        cols = slice(col, col + 512)
        acc_ref[:, cols] = acc_in[:, cols] + total((pw, qp, wq), blocks, cols)


def third_kernel(dense_ref, acc_ref, ta, tb, tc, out_ref, held, sems):
    block = block_rows(dense_ref, 6)
    copies = []
    for col in (0, 512):
        cols = slice(col, col + 512)
        base = 0
        for t_ref, n in zip((ta, tb, tc), PARTS):
            rows = slice(base, base + n)
            held[rows, cols] = (acc_ref[rows, cols] + dot(t_ref[...], block[:, cols])).astype(held.dtype)
            copy = pltpu.make_async_copy(held.at[rows, cols], out_ref.at[rows, cols], sems.at[len(copies)])
            copy.start()
            copies.append(copy)
            base += n
    for copy in copies:
        copy.wait()


def call(kernel, args, shape, dtype, name, table=False, out_space=VMEM, flops=1000, limit=8, **more):
    return pl.pallas_call(
        kernel,
        in_specs=[spec(SMEM)] * table + [spec(VMEM)] * (len(args) - table),
        out_specs=spec(out_space),
        out_shape=jax.ShapeDtypeStruct(shape, dtype),
        compiler_params=pltpu.CompilerParams(vmem_limit_bytes=limit * 1024 * 1024),
        cost_estimate=pl.CostEstimate(flops=flops, bytes_accessed=1000, transcendentals=0),
        name=name,
        **more,
    )(*args)


def shards(amps, integrals, sym_mask):
    q1, w1 = row_flip(amps, 1), row_flip(amps, 3)
    packed = call(
        pack_kernel, (sym_mask, integrals), (TILE, 2 * TILE), BF16, "pack", table=True, limit=60
    )
    table = call(table_kernel, (sym_mask,), (2, 32), jnp.int32, "table", table=True, out_space=SMEM)

    sent, packed = barrier((amps, packed))
    p1 = row_flip(sent, 4)
    pair = call(join_kernel, (packed, col_flip(packed, 2)), (2, TILE, 2 * TILE), BF16, "pair", flops=20000000000)
    quad = call(join_kernel, (pair, col_flip(pair, 1)), (4, TILE, 2 * TILE), BF16, "quad")
    r1, r2 = barrier((z_step(quad, 1), z_step(quad, 2)))
    p1, q1, w1 = barrier((p1, q1, w1))
    r3, r4 = barrier((z_step(r2, 1), z_step(r2, 2)))
    theirs = col_flip(call(three_kernel, (r1, r2, r3), (12, TILE, 2 * TILE), BF16, "three"), 1)
    dense = call(
        dense_kernel, (table, quad, r1, r2, r3, r4, theirs), (4096, 1024), BF16, "dense", table=True, flops=2000000000
    )

    pw, qp, wq = row_flip(w1, 4), row_flip(p1, 1), row_flip(q1, 3)
    acc = call(first_kernel, (dense, amps, p1, q1, w1), (1024, 1024), jnp.float32, "first")
    wq, pw, qp = (barrier((acc, v))[1] for v in (wq, pw, qp))
    a, b, _ = PARTS
    last = (row_flip(wq[:a], 4), row_flip(pw[a : a + b], 1), row_flip(qp[a + b :], 3))
    acc = call(
        second_kernel, (dense, acc, pw, qp, wq), (1024, 1024), jnp.float32, "second",
        input_output_aliases={1: 0},
    )
    return call(
        third_kernel, (dense, acc, *last), (1024, 1024), BF16, "third", out_space=pl.ANY,
        scratch_shapes=[VMEM((1024, 1024), BF16), pltpu.SemaphoreType.DMA((6,))],
    )


def solution(mesh):
    placed = (P("col", "row"), P("col", "row"), P())
    return jax.shard_map(
        shards, mesh=mesh, in_specs=placed, out_specs=P("col", "row"), check_vma=False
    )
```

```python
import jax
import jax.numpy as jnp
from jax import lax
from jax.experimental import pallas as pl
from jax.experimental.pallas import tpu as pltpu
from jax.sharding import PartitionSpec as P

TILE = 128
AB = 8
PARTS = (352, 304, 368)
VMEM = pltpu.VMEM
SMEM = pltpu.SMEM
BF16 = jnp.bfloat16
barrier = lax.optimization_barrier


def spec(space):
    return pl.BlockSpec(memory_space=space)


def row_flip(value, flip):
    return lax.ppermute(value, "row", [(i, i ^ flip) for i in range(8)])


def col_flip(value, flip):
    return lax.ppermute(value, "col", [(i, i ^ flip) for i in range(32)])


def z_step(value, by):
    return lax.ppermute(
        value, "col", [(i, (i + (4 * by if i % 2 == 0 else -4 * by)) % 32) for i in range(32)]
    )


def place():
    return lax.axis_index("row"), lax.axis_index("col")


def tile_at(index):
    return pl.ds(pl.multiple_of(index * TILE, TILE), TILE)


def pack_kernel(mask_ref, v_ref, out_ref):
    r, c = place()
    first, last, found = jnp.int32(0), jnp.int32(0), jnp.int32(0)
    for j in range(AB):
        hit = mask_ref[c, r * AB + j] > 0
        first = jnp.where(jnp.logical_and(hit, found == 0), j, first)
        last = jnp.where(hit, j, last)
        found = jnp.where(hit, 1, found)
    zero = jnp.zeros((TILE, TILE), v_ref.dtype)
    out_ref[:, :TILE] = jnp.where(found > 0, v_ref[:, tile_at(first)], zero)
    out_ref[:, TILE:] = jnp.where(last != first, v_ref[:, tile_at(last)], zero)


def table_kernel(mask_ref, out_ref):
    r, _ = place()

    @pl.loop(0, 32)
    def _(k):
        first, last = jnp.int32(AB), jnp.int32(0)
        for j in range(AB):
            hit = mask_ref[k, r * AB + j] > 0
            first = jnp.where(hit, jnp.minimum(first, j), first)
            last = jnp.where(hit, j, last)
        out_ref[0, k] = jnp.where(first == AB, 0, first)
        out_ref[1, k] = last


def join_kernel(a, b, out_ref):
    n = out_ref.shape[0] // 2
    out_ref[:n] = a[...].reshape((n,) + out_ref.shape[1:])
    out_ref[n:] = b[...].reshape((n,) + out_ref.shape[1:])


def three_kernel(a, b, c, out_ref):
    for i, ref in enumerate((a, b, c)):
        out_ref[4 * i : 4 * i + 4] = ref[...]


def dense_kernel(table_ref, quad, r1, r2, r3, r4, theirs, out_ref):
    _, c = place()
    co, xh, z = lax.rem(c, 2), lax.rem(lax.div(c, 2), 2), lax.div(c, 4)
    way = 1 - 2 * co
    out_ref[...] = jnp.zeros_like(out_ref)
    for ref, core, shift in (
        (quad, co, 0),
        (r1, co, -way),
        (r2, co, -2 * way),
        (r3, co, -3 * way),
        (r4, co, 4),
        (theirs.at[0:4], 1 - co, way),
        (theirs.at[4:8], 1 - co, 2 * way),
        (theirs.at[8:12], 1 - co, 3 * way),
    ):
        plane = lax.rem(z + shift + 8, 8)
        for j in range(4):
            k = plane * 4 + (xh ^ (j & 1)) * 2 + (core ^ (j >> 1))
            rows = tile_at(k)
            out_ref[rows, tile_at(table_ref[1, k])] = ref[j, :, TILE:]
            out_ref[rows, tile_at(table_ref[0, k])] = ref[j, :, :TILE]


def block_rows(dense_ref, flip):
    z = place()[0] ^ flip
    return dense_ref.at[pl.ds(pl.multiple_of(z * 512, 512), 512)]


def dot(a, b):
    return jnp.dot(a, b, preferred_element_type=jnp.float32)


def total(ts, blocks, cols):
    return sum(dot(t[...], block[:, cols]) for t, block in zip(ts, blocks))


def first_kernel(dense_ref, own, p1, q1, w1, acc_ref):
    blocks = [block_rows(dense_ref, flip) for flip in (0, 4, 1, 3)]
    for col in (0, 512):
        cols = slice(col, col + 512)
        acc_ref[:, cols] = total((own, p1, q1, w1), blocks, cols)


def second_kernel(dense_ref, acc_in, pw, qp, wq, acc_ref):
    blocks = [block_rows(dense_ref, flip) for flip in (7, 5, 2)]
    for col in (0, 512):
        cols = slice(col, col + 512)
        acc_ref[:, cols] = acc_in[:, cols] + total((pw, qp, wq), blocks, cols)


def third_kernel(dense_ref, acc_ref, ta, tb, tc, out_ref, held, sems):
    block = block_rows(dense_ref, 6)
    copies = []
    for col in (0, 512):
        cols = slice(col, col + 512)
        base = 0
        for t_ref, n in zip((ta, tb, tc), PARTS):
            rows = slice(base, base + n)
            held[rows, cols] = (acc_ref[rows, cols] + dot(t_ref[...], block[:, cols])).astype(held.dtype)
            copy = pltpu.make_async_copy(held.at[rows, cols], out_ref.at[rows, cols], sems.at[len(copies)])
            copy.start()
            copies.append(copy)
            base += n
    for copy in copies:
        copy.wait()


def call(kernel, args, shape, dtype, name, table=False, out_space=VMEM, flops=1000, limit=8, **more):
    return pl.pallas_call(
        kernel,
        in_specs=[spec(SMEM)] * table + [spec(VMEM)] * (len(args) - table),
        out_specs=spec(out_space),
        out_shape=jax.ShapeDtypeStruct(shape, dtype),
        compiler_params=pltpu.CompilerParams(vmem_limit_bytes=limit * 1024 * 1024),
        cost_estimate=pl.CostEstimate(flops=flops, bytes_accessed=1000, transcendentals=0),
        name=name,
        **more,
    )(*args)


def shards(amps, integrals, sym_mask):
    q1, w1 = row_flip(amps, 1), row_flip(amps, 3)
    packed = call(
        pack_kernel, (sym_mask, integrals), (TILE, 2 * TILE), BF16, "pack", table=True, limit=60
    )
    table = call(table_kernel, (sym_mask,), (2, 32), jnp.int32, "table", table=True, out_space=SMEM)

    sent, packed = barrier((amps, packed))
    p1 = row_flip(sent, 4)
    pair = call(join_kernel, (packed, col_flip(packed, 2)), (2, TILE, 2 * TILE), BF16, "pair", flops=20000000000)
    quad = call(join_kernel, (pair, col_flip(pair, 1)), (4, TILE, 2 * TILE), BF16, "quad")
    r1, r2 = barrier((z_step(quad, 1), z_step(quad, 2)))

    r3, r4 = barrier((z_step(r2, 1), z_step(r2, 2)))
    theirs = col_flip(call(three_kernel, (r1, r2, r3), (12, TILE, 2 * TILE), BF16, "three"), 1)
    dense = call(
        dense_kernel, (table, quad, r1, r2, r3, r4, theirs), (4096, 1024), BF16, "dense", table=True, flops=2000000000
    )

    pw, qp, wq = row_flip(p1, 3), row_flip(q1, 4), row_flip(w1, 1)
    acc = call(first_kernel, (dense, amps, p1, q1, w1), (1024, 1024), jnp.float32, "first")
    wq, pw, qp = (barrier((acc, v))[1] for v in (wq, pw, qp))
    a, b, _ = PARTS
    last = (row_flip(wq[:a], 4), row_flip(pw[a : a + b], 1), row_flip(qp[a + b :], 3))
    acc = call(
        second_kernel, (dense, acc, pw, qp, wq), (1024, 1024), jnp.float32, "second",
        input_output_aliases={1: 0},
    )
    return call(
        third_kernel, (dense, acc, *last), (1024, 1024), BF16, "third", out_space=pl.ANY,
        scratch_shapes=[VMEM((1024, 1024), BF16), pltpu.SemaphoreType.DMA((6,))],
    )


def solution(mesh):
    placed = (P("col", "row"), P("col", "row"), P())
    return jax.shard_map(
        shards, mesh=mesh, in_specs=placed, out_specs=P("col", "row"), check_vma=False
    )
```

```python
import jax
import jax.numpy as jnp
from jax import lax
from jax.experimental import pallas as pl
from jax.experimental.pallas import tpu as pltpu
from jax.sharding import PartitionSpec as P

TILE = 128
AB = 8
PARTS = (352, 304, 368)
VMEM = pltpu.VMEM
SMEM = pltpu.SMEM
BF16 = jnp.bfloat16
barrier = lax.optimization_barrier


def spec(space):
    return pl.BlockSpec(memory_space=space)


def row_flip(value, flip):
    return lax.ppermute(value, "row", [(i, i ^ flip) for i in range(8)])


def col_flip(value, flip):
    return lax.ppermute(value, "col", [(i, i ^ flip) for i in range(32)])


def z_step(value, by):
    return lax.ppermute(
        value, "col", [(i, (i + (4 * by if i % 2 == 0 else -4 * by)) % 32) for i in range(32)]
    )


def place():
    return lax.axis_index("row"), lax.axis_index("col")


def tile_at(index):
    return pl.ds(pl.multiple_of(index * TILE, TILE), TILE)


def pack_kernel(mask_ref, v_ref, out_ref):
    r, c = place()
    first, last, found = jnp.int32(0), jnp.int32(0), jnp.int32(0)
    for j in range(AB):
        hit = mask_ref[c, r * AB + j] > 0
        first = jnp.where(jnp.logical_and(hit, found == 0), j, first)
        last = jnp.where(hit, j, last)
        found = jnp.where(hit, 1, found)
    zero = jnp.zeros((TILE, TILE), v_ref.dtype)
    out_ref[:, :TILE] = jnp.where(found > 0, v_ref[:, tile_at(first)], zero)
    out_ref[:, TILE:] = jnp.where(last != first, v_ref[:, tile_at(last)], zero)


def table_kernel(mask_ref, out_ref):
    r, _ = place()

    @pl.loop(0, 32)
    def _(k):
        first, last = jnp.int32(AB), jnp.int32(0)
        for j in range(AB):
            hit = mask_ref[k, r * AB + j] > 0
            first = jnp.where(hit, jnp.minimum(first, j), first)
            last = jnp.where(hit, j, last)
        out_ref[0, k] = jnp.where(first == AB, 0, first)
        out_ref[1, k] = last


def join_kernel(a, b, out_ref):
    n = out_ref.shape[0] // 2
    out_ref[:n] = a[...].reshape((n,) + out_ref.shape[1:])
    out_ref[n:] = b[...].reshape((n,) + out_ref.shape[1:])


def three_kernel(a, b, c, out_ref):
    for i, ref in enumerate((a, b, c)):
        out_ref[4 * i : 4 * i + 4] = ref[...]


def dense_kernel(table_ref, quad, r1, r2, r3, r4, theirs, out_ref):
    _, c = place()
    co, xh, z = lax.rem(c, 2), lax.rem(lax.div(c, 2), 2), lax.div(c, 4)
    way = 1 - 2 * co
    out_ref[...] = jnp.zeros_like(out_ref)
    for ref, core, shift in (
        (quad, co, 0),
        (r1, co, -way),
        (r2, co, -2 * way),
        (r3, co, -3 * way),
        (r4, co, 4),
        (theirs.at[0:4], 1 - co, way),
        (theirs.at[4:8], 1 - co, 2 * way),
        (theirs.at[8:12], 1 - co, 3 * way),
    ):
        plane = lax.rem(z + shift + 8, 8)
        for j in range(4):
            k = plane * 4 + (xh ^ (j & 1)) * 2 + (core ^ (j >> 1))
            rows = tile_at(k)
            out_ref[rows, tile_at(table_ref[1, k])] = ref[j, :, TILE:]
            out_ref[rows, tile_at(table_ref[0, k])] = ref[j, :, :TILE]


def block_rows(dense_ref, flip):
    z = place()[0] ^ flip
    return dense_ref.at[pl.ds(pl.multiple_of(z * 512, 512), 512)]


def dot(a, b):
    return jnp.dot(a, b, preferred_element_type=jnp.float32)


def total(ts, blocks, cols):
    return sum(dot(t[...], block[:, cols]) for t, block in zip(ts, blocks))


def first_kernel(dense_ref, own, p1, q1, w1, acc_ref):
    blocks = [block_rows(dense_ref, flip) for flip in (0, 4, 1, 3)]
    for col in (0, 512):
        cols = slice(col, col + 512)
        acc_ref[:, cols] = total((own, p1, q1, w1), blocks, cols)


def second_kernel(dense_ref, acc_in, pw, qp, wq, acc_ref):
    blocks = [block_rows(dense_ref, flip) for flip in (7, 5, 2)]
    for col in (0, 512):
        cols = slice(col, col + 512)
        acc_ref[:, cols] = acc_in[:, cols] + total((pw, qp, wq), blocks, cols)


def third_kernel(dense_ref, acc_ref, ta, tb, tc, out_ref, held, sems):
    block = block_rows(dense_ref, 6)
    copies = []
    for col in (0, 512):
        cols = slice(col, col + 512)
        base = 0
        for t_ref, n in zip((ta, tb, tc), PARTS):
            rows = slice(base, base + n)
            held[rows, cols] = (acc_ref[rows, cols] + dot(t_ref[...], block[:, cols])).astype(held.dtype)
            copy = pltpu.make_async_copy(held.at[rows, cols], out_ref.at[rows, cols], sems.at[len(copies)])
            copy.start()
            copies.append(copy)
            base += n
    for copy in copies:
        copy.wait()


def call(kernel, args, shape, dtype, name, table=False, out_space=VMEM, flops=1000, limit=8, **more):
    return pl.pallas_call(
        kernel,
        in_specs=[spec(SMEM)] * table + [spec(VMEM)] * (len(args) - table),
        out_specs=spec(out_space),
        out_shape=jax.ShapeDtypeStruct(shape, dtype),
        compiler_params=pltpu.CompilerParams(vmem_limit_bytes=limit * 1024 * 1024),
        cost_estimate=pl.CostEstimate(flops=flops, bytes_accessed=1000, transcendentals=0),
        name=name,
        **more,
    )(*args)


def shards(amps, integrals, sym_mask):
    q1, w1 = row_flip(amps, 1), row_flip(amps, 3)
    packed = call(
        pack_kernel, (sym_mask, integrals), (TILE, 2 * TILE), BF16, "pack", table=True, limit=60
    )
    table = call(table_kernel, (sym_mask,), (2, 32), jnp.int32, "table", table=True, out_space=SMEM)

    sent, packed = barrier((amps, packed))
    p1 = row_flip(sent, 4)
    pair = call(join_kernel, (packed, col_flip(packed, 2)), (2, TILE, 2 * TILE), BF16, "pair", flops=20000000000, limit=60)
    quad = call(join_kernel, (pair, col_flip(pair, 1)), (4, TILE, 2 * TILE), BF16, "quad")
    r1, r2 = barrier((z_step(quad, 1), z_step(quad, 2)))
    p1, q1, w1 = barrier((p1, q1, w1))
    r3, r4 = barrier((z_step(r2, 1), z_step(r2, 2)))
    theirs = col_flip(call(three_kernel, (r1, r2, r3), (12, TILE, 2 * TILE), BF16, "three"), 1)
    dense = call(
        dense_kernel, (table, quad, r1, r2, r3, r4, theirs), (4096, 1024), BF16, "dense", table=True, flops=2000000000
    )

    pw, qp, wq = row_flip(w1, 4), row_flip(p1, 1), row_flip(q1, 3)
    acc = call(first_kernel, (dense, amps, p1, q1, w1), (1024, 1024), jnp.float32, "first")
    wq, pw, qp = (barrier((acc, v))[1] for v in (wq, pw, qp))
    a, b, _ = PARTS
    last = (row_flip(wq[:a], 4), row_flip(pw[a : a + b], 1), row_flip(qp[a + b :], 3))
    acc = call(
        second_kernel, (dense, acc, pw, qp, wq), (1024, 1024), jnp.float32, "second",
        input_output_aliases={1: 0},
    )
    return call(
        third_kernel, (dense, acc, *last), (1024, 1024), BF16, "third", out_space=pl.ANY,
        scratch_shapes=[VMEM((1024, 1024), BF16), pltpu.SemaphoreType.DMA((6,))],
    )


def solution(mesh):
    placed = (P("col", "row"), P("col", "row"), P())
    return jax.shard_map(
        shards, mesh=mesh, in_specs=placed, out_specs=P("col", "row"), check_vma=False
    )
```
